32 devices in a mesh: row: 8 (over z, x), col: 4 (over y, core).
Axes of the slice: x: 2, y: 2, z: 4, core: 2. Of those that a mesh axis runs over, the one named last changes fastest.
Arguments:
- feat: bfloat16 [256, 128, 256], P('row', 'col'), may hold values from -6 to 6
- noise_fine: float32 [256, 128, 256], P('row', 'col'), may hold values from -0.5 to 0.5
- noise_coarse: float32 [128, 64, 256], P('row', 'col'), may hold values from -0.5 to 0.5
- w_post: bfloat16 [2304, 256], replicated, may hold values from -0.125 to 0.125
- w_coarse: bfloat16 [2304, 256], replicated, may hold values from -0.125 to 0.125
- w_prior: bfloat16 [2304, 512], replicated, may hold values from -0.125 to 0.125
Outputs:
- grad_feat: bfloat16 [256, 128, 256], P('row', 'col')
- grad_post: float32 [589824], P(('row', 'col'))
- grad_coarse: float32 [589824], P(('row', 'col'))
- grad_prior: float32 [1179648], P(('row', 'col'))
The draws below stay inside these ranges and needn't reach their ends.
All inputs are finite; a program needn't handle non-finite values.
Results may differ from the reference program's by a relative error of at most 0.0075.
Values may be sent and summed in bfloat16 or wider, within the bound.
A program may use at most 128 MiB of HBM per device.

```python
import math
import jax
import jax.numpy as jnp

C = 256
H = 256
W = 128
H2 = 128
W2 = 64


def with_spikes(entries, own_key, source, target, parts, factor):
    def block_of(position):
        return (jnp.arange(entries.shape[position]) // (entries.shape[position] // parts)).reshape((-1,) + (1,) * (entries.ndim - 1 - position))

    first = jax.random.permutation(own_key, parts)[block_of(target)]
    far = (block_of(target) + parts // 2) % parts
    return jnp.where((block_of(source) == first) | (block_of(source) == far), factor * entries, entries)


def steps_of(rng, shape, shards, smallest, largest):
    level = 1.0
    for position, shards_of in shards:
        heights = jax.random.uniform(jax.random.fold_in(jax.random.fold_in(rng, 6), position), (shards_of,), jnp.float32, smallest / len(shards), largest / len(shards))
        level = level * jnp.repeat(jnp.exp(heights), shape[position] // shards_of).reshape((-1,) + (1,) * (len(shape) - 1 - position))
    return level


def centred(rng, dims, width, bound, cuts=(), held_as=jnp.bfloat16):
    loudness = steps_of(rng, dims, cuts, -0.22, 0.18) if cuts else 1.0
    drawn = jax.random.normal(rng, dims, jnp.float32) * width * loudness
    return jnp.minimum(jnp.maximum(drawn, -bound), bound).astype(held_as)


def bell_draw_with(stream_key, shape, scale, limit, pieces, heavy, held_as=jnp.bfloat16):
    entries = scale * jax.random.normal(stream_key, shape, jnp.float32)
    if pieces:
        entries = entries * steps_of(stream_key, shape, pieces, -0.22, 0.18)
    return jnp.clip(with_spikes(entries, jax.random.fold_in(stream_key, 3), *heavy), -limit, limit).astype(held_as)


def setup_inputs(seed: int = 0) -> dict:
    streams_of = jax.random.split(jax.random.key(seed), 7)
    return {
        "feat": bell_draw_with(streams_of[0], (H, W, C), 1.0, 6.0, ((0, 8), (1, 4)), (0, 2, 8, 2.0)),
        "noise_fine": jnp.clip(jax.random.uniform(streams_of[1], (H, W, C), jnp.float32, -0.5, 0.5) * steps_of(streams_of[1], (H, W, C), ((0, 8), (1, 4)), -0.4, 0.0), -0.5, 0.5),
        "noise_coarse": jnp.clip(jax.random.uniform(streams_of[2], (H2, W2, C), jnp.float32, -0.5, 0.5) * steps_of(streams_of[2], (H2, W2, C), ((0, 8), (1, 4)), -0.4, 0.0), -0.5, 0.5),
        "w_post": centred(streams_of[3], (9 * C, C), (9 * C) ** -0.5, 0.125),
        "w_coarse": centred(streams_of[4], (9 * C, C), (9 * C) ** -0.5, 0.125),
        "w_prior": centred(streams_of[5], (9 * C, 2 * C), (9 * C) ** -0.5, 0.125),
    }


def conv_taps(field, weight):
    size_r, size_c, chans = field.shape
    padded = jnp.pad(field, ((1, 1), (1, 1), (0, 0)))
    total = jnp.zeros((size_r * size_c, weight.shape[1]), jnp.float32)
    for tap_row in range(3):
        for tap_col in range(3):
            index = 3 * tap_row + tap_col
            piece = padded[tap_row:tap_row + size_r, tap_col:tap_col + size_c].reshape(-1, chans)
            total = total + jnp.dot(piece, weight[index * chans:(index + 1) * chans], preferred_element_type=jnp.float32)
    return total.reshape(size_r, size_c, weight.shape[1])

def conv_back(grad, weight):
    size_r, size_c, chans_g = grad.shape
    chans_in = weight.shape[0] // 9
    padded = jnp.pad(grad, ((1, 1), (1, 1), (0, 0)))
    total = jnp.zeros((size_r * size_c, chans_in), jnp.float32)
    for tap_row in range(3):
        for tap_col in range(3):
            index = 3 * tap_row + tap_col
            piece = padded[2 - tap_row:2 - tap_row + size_r, 2 - tap_col:2 - tap_col + size_c].reshape(-1, chans_g)
            total = total + jnp.dot(piece, weight[index * chans_in:(index + 1) * chans_in].T, preferred_element_type=jnp.float32)
    return total.reshape(size_r, size_c, chans_in)

def weight_grad(field, grad):
    size_r, size_c, chans = field.shape
    padded = jnp.pad(field, ((1, 1), (1, 1), (0, 0)))
    flat_grad = grad.reshape(-1, grad.shape[-1])
    blocks = []
    for tap_row in range(3):
        for tap_col in range(3):
            piece = padded[tap_row:tap_row + size_r, tap_col:tap_col + size_c].reshape(-1, chans)
            blocks.append(jnp.dot(piece.T, flat_grad, preferred_element_type=jnp.float32))
    return jnp.concatenate(blocks, axis=0)

def repeat_two(field):
    return jnp.repeat(jnp.repeat(field, 2, axis=0), 2, axis=1)

def reference(feat, noise_fine, noise_coarse, w_post, w_coarse, w_prior):
    full_r, full_c, chans = feat.shape
    grad_scale = 1.0 / math.sqrt(full_r * full_c)
    fine = conv_taps(feat, w_post) + noise_fine
    pooled = fine.reshape(full_r // 2, 2, full_c // 2, 2, chans).mean(axis=(1, 3)).astype(jnp.bfloat16)
    coarse = conv_taps(pooled, w_coarse) + noise_coarse
    context = repeat_two(coarse.astype(jnp.bfloat16))
    prior = conv_taps(context, w_prior)
    prior_mean = prior[..., :chans]
    raw_scale = prior[..., chans:]
    prior_scale = jax.nn.softplus(raw_scale) + 0.5
    deviation = fine - prior_mean
    residual_term = deviation / (prior_scale * prior_scale)
    scale_term = 1.0 / prior_scale - deviation * deviation / (prior_scale * prior_scale * prior_scale)
    dprior = jnp.concatenate([-residual_term, scale_term * jax.nn.sigmoid(raw_scale)], axis=-1).astype(jnp.bfloat16)
    grad_prior = weight_grad(context, dprior) * grad_scale
    back_context = conv_back(dprior, w_prior)
    gcoarse = (coarse + back_context.reshape(full_r // 2, 2, full_c // 2, 2, chans).sum(axis=(1, 3))).astype(jnp.bfloat16)
    grad_coarse = weight_grad(pooled, gcoarse) * grad_scale
    back_pooled = conv_back(gcoarse, w_coarse)
    gfine = (residual_term + 0.25 * repeat_two(back_pooled)).astype(jnp.bfloat16)
    grad_post = weight_grad(feat, gfine) * grad_scale
    grad_feat = conv_back(gfine, w_post).astype(jnp.bfloat16)
    return (grad_feat, grad_post.reshape(-1), grad_coarse.reshape(-1), grad_prior.reshape(-1))
```

```python
import functools
import math

import jax
import jax.numpy as jnp
from jax import lax
from jax.experimental import pallas as pl
from jax.experimental.pallas import tpu as pltpu
from jax.sharding import PartitionSpec as P

F32 = jnp.float32
BF16 = jnp.bfloat16
EDGE = 8


LANES = 128


def put(ref, at, values):
    for d in range(ref.shape[0]):
        ref[d, at, :] = values[:, d * LANES : (d + 1) * LANES]


def get(ref, at):
    return jnp.concatenate([ref[d, at, :] for d in range(ref.shape[0])], axis=1)


def tile_kernel(
    dims,
    feat,
    noise_fine,
    noise_coarse,
    w_post,
    w_coarse,
    w_prior,
    grad_feat,
    grad_post,
    grad_coarse,
    grad_prior,
    fine,
    err,
    coarse,
    mix,
    s_feat,
    s_pool,
    s_ctx,
    s_dpr,
    s_gco,
    s_gfi,
    x_feat,
    x_pool,
    x_ctx,
    x_dpr,
    x_gco,
    x_gfi,
    edge_fine,
    edge_coarse,
    edge_dpr,
    sems,
):
    rows, cols, chans, scale, n_row, n_col = dims
    half_rows, half_cols = rows // 2, cols // 2
    r = lax.axis_index("row")
    c = lax.axis_index("col")
    has_up, has_down = r > 0, r < n_row - 1
    has_left, has_right = c > 0, c < n_col - 1
    sides = (
        (has_up, {"row": r - 1}),
        (has_down, {"row": r + 1}),
        (has_left, {"col": c - 1}),
        (has_right, {"col": c + 1}),
    )
    edge_fine[...] = jnp.zeros_like(edge_fine)
    edge_coarse[...] = jnp.zeros_like(edge_coarse)
    edge_dpr[...] = jnp.zeros_like(edge_dpr)
    for x, width, height in (
        (x_feat, cols, rows),
        (x_pool, half_cols, half_rows),
        (x_ctx, cols, rows),
        (x_dpr, cols, rows),
        (x_gco, half_cols, half_rows),
        (x_gfi, cols, rows),
    ):
        x[0:width, :] = jnp.zeros((width, x.shape[1]), x.dtype)
        x[(height + 1) * width :, :] = jnp.zeros((width, x.shape[1]), x.dtype)

    barrier = pltpu.get_barrier_semaphore()
    for has, device in sides:
        @pl.when(has)
        def _(device=device):
            pl.semaphore_signal(
                barrier, inc=1, device_id=device, device_id_type=pl.DeviceIdType.MESH
            )
    pl.semaphore_wait(barrier, sum(has.astype(jnp.int32) for has, _device in sides))

    def exchange(index, s, x, edges, slot, height, width, work_1=None, work_2=None):
        stride = width + 2 * EDGE
        depth = s.shape[0] * LANES

        def copy(src, dst, k, device):
            return pltpu.make_async_remote_copy(
                src_ref=src,
                dst_ref=dst,
                send_sem=sems.at[index, k],
                recv_sem=sems.at[index, 4 + k],
                device_id=device,
                device_id_type=pl.DeviceIdType.MESH,
            )

        edges[slot, 0] = get(s, pl.ds(EDGE, height, stride=stride)).astype(BF16)
        edges[slot, 1] = get(s, pl.ds(EDGE + width - 1, height, stride=stride)).astype(BF16)
        leftward = copy(edges.at[slot, 0], edges.at[slot, 3], 0, {"col": c - 1})
        rightward = copy(edges.at[slot, 1], edges.at[slot, 2], 1, {"col": c + 1})
        pl.when(has_left)(leftward.start)
        pl.when(has_right)(rightward.start)
        for i in range(height):
            x[pl.ds((i + 1) * width, width), depth : 2 * depth] = get(
                s, pl.ds(i * stride + EDGE, width)
            ).astype(BF16)
        if work_1 is not None:
            work_1()

        @pl.when(has_left)
        def _():
            leftward.wait_send()
            rightward.wait_recv()

        @pl.when(has_right)
        def _():
            rightward.wait_send()
            leftward.wait_recv()

        put(s, pl.ds(EDGE - 1, height, stride=stride), edges[slot, 2].astype(F32))
        put(s, pl.ds(EDGE + width, height, stride=stride), edges[slot, 3].astype(F32))
        order = [0, height - 1] + list(range(1, height - 1))
        upward = copy(
            x.at[pl.ds(width, width)], x.at[pl.ds((height + 1) * width, width)], 2, {"row": r - 1}
        )
        downward = copy(
            x.at[pl.ds(height * width, width)], x.at[pl.ds(0, width)], 3, {"row": r + 1}
        )
        for n, i in enumerate(order):
            for b in (0, 2):
                x[pl.ds((i + 1) * width, width), b * depth : (b + 1) * depth] = get(
                    s, pl.ds(i * stride + EDGE - 1 + b, width)
                ).astype(BF16)
            if n == 1:
                pl.when(has_up)(upward.start)
                pl.when(has_down)(downward.start)
        if work_2 is not None:
            work_2()

        @pl.when(has_up)
        def _():
            upward.wait_send()
            downward.wait_recv()

        @pl.when(has_down)
        def _():
            downward.wait_send()
            upward.wait_recv()

    def conv(x, w, start, size, width):
        k = w.shape[0] // 3
        total = None
        for a in range(3):
            part = jnp.dot(
                x[pl.ds(start + a * width, size), :],
                w[a * k : (a + 1) * k, :],
                preferred_element_type=F32,
            )
            total = part if total is None else total + part
        return total

    def conv_back(x, w, start, size, width):
        k = w.shape[0] // 9
        depth = w.shape[1]
        total = None
        for a in range(3):
            for b in range(3):
                tap = 3 * (2 - a) + (2 - b)
                part = lax.dot_general(
                    x[pl.ds(start + a * width, size), b * depth : (b + 1) * depth],
                    w[tap * k : (tap + 1) * k, :],
                    (((1,), (1,)), ((), ())),
                    preferred_element_type=F32,
                )
                total = part if total is None else total + part
        return total

    def weight_grad(x, g, out, height, width, taps):
        depth = x.shape[1] // 3
        g_depth = g.shape[1] // 3
        size = height * width
        own = g[pl.ds(width, size), g_depth : 2 * g_depth]
        for a in taps:
            for b in range(3):
                tap = 3 * a + b
                out[tap * depth : (tap + 1) * depth, :] = scale * lax.dot_general(
                    x[pl.ds(a * width, size), b * depth : (b + 1) * depth],
                    own,
                    (((0,), (0,)), ((), ())),
                    preferred_element_type=F32,
                )

    lines = 8
    block = lines * cols
    half_block = block // 4

    def pool_sum(values):
        paired = values.reshape(lines // 2, 2, cols, chans)
        put(mix, pl.ds(0, block // 2), (paired[:, 0] + paired[:, 1]).reshape(block // 2, chans))
        return get(mix, pl.ds(0, half_block, stride=2)) + get(mix, pl.ds(1, half_block, stride=2))

    def repeat_columns(values):
        put(mix, pl.ds(0, half_rows * half_cols, stride=2), values)
        put(mix, pl.ds(1, half_rows * half_cols, stride=2), values)

    fine_stride = cols + 2 * EDGE
    half_stride = half_cols + 2 * EDGE

    for i in range(rows):
        put(s_feat, pl.ds(i * fine_stride + EDGE, cols), feat[pl.ds(i * cols, cols), :].astype(F32))
    exchange(0, s_feat, x_feat, edge_fine, 0, rows, cols)

    for m in range(rows // lines):
        values = conv(x_feat, w_post, m * block, block, cols) + noise_fine[pl.ds(m * block, block), :]
        fine[pl.ds(m * block, block), :] = values
        pooled = (0.25 * pool_sum(values)).astype(BF16).astype(F32)
        for i in range(lines // 2):
            at = pl.ds((m * lines // 2 + i) * half_stride + EDGE, half_cols)
            put(s_pool, at, pooled[i * half_cols : (i + 1) * half_cols])
    exchange(1, s_pool, x_pool, edge_coarse, 0, half_rows, half_cols)

    values = conv(x_pool, w_coarse, 0, half_rows * half_cols, half_cols) + noise_coarse[...]
    coarse[...] = values
    repeat_columns(values.astype(BF16).astype(F32))
    for i in range(rows):
        put(s_ctx, pl.ds(i * fine_stride + EDGE, cols), get(mix, pl.ds(i // 2 * cols, cols)))
    exchange(2, s_ctx, x_ctx, edge_fine, 1, rows, cols)

    for m in range(rows // lines):
        prior = conv(x_ctx, w_prior, m * block, block, cols)
        raw = prior[:, chans:]
        small = jnp.exp(-jnp.abs(raw))
        sigma = jnp.maximum(raw, 0.0) + jnp.log1p(small) + 0.5
        gate = jnp.where(raw >= 0, 1.0, small) / (1.0 + small)
        inverse = 1.0 / sigma
        deviation = fine[pl.ds(m * block, block), :] - prior[:, :chans]
        ratio = deviation * inverse
        residual = ratio * inverse
        err[pl.ds(m * block, block), :] = residual
        slope = (inverse - ratio * ratio * inverse) * gate
        for i in range(lines):
            at = pl.ds((m * lines + i) * fine_stride + EDGE, cols)
            here = slice(i * cols, (i + 1) * cols)
            both = jnp.concatenate([-residual[here], slope[here]], axis=1)
            put(s_dpr, at, both.astype(BF16).astype(F32))
    exchange(
        3,
        s_dpr,
        x_dpr,
        edge_dpr,
        0,
        rows,
        cols,
        lambda: weight_grad(x_ctx, x_dpr, grad_prior, rows, cols, (0, 1)),
        lambda: weight_grad(x_ctx, x_dpr, grad_prior, rows, cols, (2,)),
    )

    for m in range(rows // lines):
        back = pool_sum(conv_back(x_dpr, w_prior, m * block, block, cols))
        g = (coarse[pl.ds(m * half_block, half_block), :] + back).astype(BF16).astype(F32)
        for i in range(lines // 2):
            at = pl.ds((m * lines // 2 + i) * half_stride + EDGE, half_cols)
            put(s_gco, at, g[i * half_cols : (i + 1) * half_cols])
    exchange(
        4,
        s_gco,
        x_gco,
        edge_coarse,
        1,
        half_rows,
        half_cols,
        lambda: weight_grad(x_pool, x_gco, grad_coarse, half_rows, half_cols, (0, 1)),
        lambda: weight_grad(x_pool, x_gco, grad_coarse, half_rows, half_cols, (2,)),
    )

    repeat_columns(0.25 * conv_back(x_gco, w_coarse, 0, half_rows * half_cols, half_cols))
    for i in range(rows):
        total = err[pl.ds(i * cols, cols), :] + get(mix, pl.ds(i // 2 * cols, cols))
        put(s_gfi, pl.ds(i * fine_stride + EDGE, cols), total.astype(BF16).astype(F32))
    exchange(
        5,
        s_gfi,
        x_gfi,
        edge_fine,
        2,
        rows,
        cols,
        lambda: weight_grad(x_feat, x_gfi, grad_post, rows, cols, (0, 1)),
        lambda: weight_grad(x_feat, x_gfi, grad_post, rows, cols, (2,)),
    )
    for m in range(rows // lines):
        grad_feat[pl.ds(m * block, block), :] = conv_back(
            x_gfi, w_post, m * block, block, cols
        ).astype(BF16)


def reduce_scatter(partials, n_row, n_col, bits):
    count = n_row * n_col
    me = lax.axis_index("row") * n_col + lax.axis_index("col")
    total_bits = count.bit_length() - 1
    value = partials.reshape((2,) * total_bits + partials.shape[1:])
    left = list(range(total_bits))
    for bit in bits:
        dim = left.index(total_bits - 1 - bit)
        mine = (me >> bit) & 1
        away = lax.dynamic_slice_in_dim(value, 1 - mine, 1, dim).astype(BF16)
        away = lax.squeeze(away, (dim,))
        got = lax.ppermute(away, ("row", "col"), [(i, i ^ (1 << bit)) for i in range(count)])
        kept = lax.squeeze(lax.dynamic_slice_in_dim(value, mine, 1, dim), (dim,))
        value = kept + got.astype(F32)
        left.remove(total_bits - 1 - bit)
    return value.reshape(-1)


def on_device(sizes, feat, noise_fine, noise_coarse, w_post, w_coarse, w_prior):
    n_row, n_col = sizes
    rows, cols, chans = feat.shape
    half_rows, half_cols = rows // 2, cols // 2
    scale = 1.0 / math.sqrt(rows * n_row * cols * n_col)
    cells, half_cells = rows * cols, half_rows * half_cols
    vmem = pl.BlockSpec(memory_space=pltpu.VMEM)

    def padded(height, width, depth):
        return pltpu.VMEM((depth // LANES, height * (width + 2 * EDGE), LANES), F32)

    def columns(height, width, depth):
        return pltpu.VMEM(((height + 2) * width, 3 * depth), BF16)

    dims = (rows, cols, chans, scale, n_row, n_col)
    grad_feat, grad_post, grad_coarse, grad_prior = pl.pallas_call(
        functools.partial(tile_kernel, dims),
        out_shape=(
            jax.ShapeDtypeStruct((cells, chans), BF16),
            jax.ShapeDtypeStruct(w_post.shape, F32),
            jax.ShapeDtypeStruct(w_coarse.shape, F32),
            jax.ShapeDtypeStruct(w_prior.shape, F32),
        ),
        in_specs=[vmem] * 6,
        out_specs=(vmem,) * 4,
        scratch_shapes=[
            pltpu.VMEM((cells, chans), F32),
            pltpu.VMEM((cells, chans), F32),
            pltpu.VMEM((half_cells, chans), F32),
            pltpu.VMEM((chans // LANES, 2 * half_cells, LANES), F32),
            padded(rows, cols, chans),
            padded(half_rows, half_cols, chans),
            padded(rows, cols, chans),
            padded(rows, cols, 2 * chans),
            padded(half_rows, half_cols, chans),
            padded(rows, cols, chans),
            columns(rows, cols, chans),
            columns(half_rows, half_cols, chans),
            columns(rows, cols, chans),
            columns(rows, cols, 2 * chans),
            columns(half_rows, half_cols, chans),
            columns(rows, cols, chans),
            pltpu.VMEM((3, 4, rows, chans), BF16),
            pltpu.VMEM((2, 4, half_rows, chans), BF16),
            pltpu.VMEM((1, 4, rows, 2 * chans), BF16),
            pltpu.SemaphoreType.DMA((6, 8)),
        ],
        compiler_params=pltpu.CompilerParams(
            collective_id=0, has_side_effects=True, vmem_limit_bytes=60000 * 1024
        ),
    )(
        feat.reshape(cells, chans),
        noise_fine.reshape(cells, chans),
        noise_coarse.reshape(half_cells, chans),
        w_post,
        w_coarse,
        w_prior,
    )
    count = n_row * n_col
    bits = list(range(count.bit_length() - 1))
    core, rest = bits[0], bits[1:]

    def shard(grad):
        return grad.reshape(count, -1, grad.shape[1])

    outs = []
    for n, grad in enumerate((grad_post, grad_coarse, grad_prior)):
        order = [core] + rest[n:] + rest[:n]
        outs.append(reduce_scatter(shard(grad), n_row, n_col, order))
    return (grad_feat.reshape(rows, cols, chans), *outs)


def solution(mesh):
    sizes = (mesh.shape["row"], mesh.shape["col"])
    return jax.shard_map(
        functools.partial(on_device, sizes),
        mesh=mesh,
        in_specs=(
            P("row", "col", None),
            P("row", "col", None),
            P("row", "col", None),
            P(),
            P(),
            P(),
        ),
        out_specs=(P("row", "col", None), P(("row", "col")), P(("row", "col")), P(("row", "col"))),
        check_vma=False,
    )
```

```python
import functools
import math

import jax
import jax.numpy as jnp
from jax import lax
from jax.experimental import pallas as pl
from jax.experimental.pallas import tpu as pltpu
from jax.sharding import PartitionSpec as P

F32 = jnp.float32
BF16 = jnp.bfloat16
EDGE = 8


LANES = 128


def put(ref, at, values):
    for d in range(ref.shape[0]):
        ref[d, at, :] = values[:, d * LANES : (d + 1) * LANES]


def get(ref, at):
    return jnp.concatenate([ref[d, at, :] for d in range(ref.shape[0])], axis=1)


def tile_kernel(
    dims,
    feat,
    noise_fine,
    noise_coarse,
    w_post,
    w_coarse,
    w_prior,
    grad_feat,
    out_post,
    out_coarse,
    out_prior,
    fine,
    err,
    coarse,
    mix,
    s_feat,
    s_pool,
    s_dpr,
    x_feat,
    x_pool,
    x_ctx,
    x_dpr,
    x_gco,
    x_gfi,
    edge_fine,
    edge_coarse,
    edge_dpr,
    sums,
    outgoing,
    incoming,
    sems,
    chain_sems,
):
    s_ctx = s_gfi = s_feat
    s_gco = s_pool
    rows, cols, chans, scale, n_row, n_col = dims
    half_rows, half_cols = rows // 2, cols // 2
    r = lax.axis_index("row")
    c = lax.axis_index("col")
    has_up, has_down = r > 0, r < n_row - 1
    has_left, has_right = c > 0, c < n_col - 1
    sides = (
        (has_up, {"row": r - 1}),
        (has_down, {"row": r + 1}),
        (has_left, {"col": c - 1}),
        (has_right, {"col": c + 1}),
    )
    edge_fine[...] = jnp.zeros_like(edge_fine)
    edge_coarse[...] = jnp.zeros_like(edge_coarse)
    edge_dpr[...] = jnp.zeros_like(edge_dpr)
    for x, width, height in (
        (x_feat, cols, rows),
        (x_pool, half_cols, half_rows),
        (x_ctx, cols, rows),
        (x_dpr, cols, rows),
        (x_gco, half_cols, half_rows),
        (x_gfi, cols, rows),
    ):
        x[0:width, :] = jnp.zeros((width, x.shape[1]), x.dtype)
        x[(height + 1) * width :, :] = jnp.zeros((width, x.shape[1]), x.dtype)

    barrier = pltpu.get_barrier_semaphore()
    for has, device in sides:
        @pl.when(has)
        def _(device=device):
            pl.semaphore_signal(
                barrier, inc=1, device_id=device, device_id_type=pl.DeviceIdType.MESH
            )
    count = n_row * n_col
    bits = count.bit_length() - 1
    col_bits = n_col.bit_length() - 1
    me = r * n_col + c

    def bit_of(b):
        return me // 2**b % 2

    def partner(b):
        if b < col_bits:
            return {"col": c + 2**b * (1 - 2 * bit_of(b))}
        return {"row": r + 2 ** (b - col_bits) * (1 - 2 * bit_of(b))}

    for b in range(bits):
        pl.semaphore_signal(
            barrier, inc=1, device_id=partner(b), device_id_type=pl.DeviceIdType.MESH
        )
    pl.semaphore_wait(barrier, bits + sum(has.astype(jnp.int32) for has, _device in sides))

    def each(n, body):
        if n <= 16:
            for j in range(n):
                body(j)
        else:
            pl.loop(0, n)(body)

    def chain(number, order, out, out_at):
        acc, send, recv = sums[number], outgoing[number], incoming[number]
        state = {"step": 0, "copy": None}

        def offset(k):
            return count - (count >> k)

        def step():
            k = state["step"]
            if k > bits:
                return
            state["step"] = k + 1
            if k > 0:
                state["copy"].wait()
            if k == bits:
                out[:, out_at] = acc[me] + recv[offset(k - 1)].astype(F32)
                return
            bit = order[k]
            free = [b for b in range(bits) if b not in order[:k]]
            rest = [b for b in free if b != bit]
            place = free.index(bit)
            fixed = sum((bit_of(b) * 2**b for b in order[:k]), 0)
            n = count >> (k + 1)

            def value(j, choice):
                index = fixed + choice * 2**bit
                for q, b in enumerate(rest):
                    index = index + j // 2**q % 2 * 2**b
                total = acc[index]
                if k > 0:
                    slot = j // 2**place * 2 ** (place + 1) + choice * 2**place + j % 2**place
                    total = total + recv[offset(k - 1) + slot].astype(F32)
                return index, total

            def fill(j):
                send[offset(k) + j] = value(j, 1 - bit_of(bit))[1].astype(BF16)

            each(n, fill)
            state["copy"] = pltpu.make_async_remote_copy(
                src_ref=send.at[pl.ds(offset(k), n)],
                dst_ref=recv.at[pl.ds(offset(k), n)],
                send_sem=chain_sems.at[number, k, 0],
                recv_sem=chain_sems.at[number, k, 1],
                device_id=partner(bit),
                device_id_type=pl.DeviceIdType.MESH,
            )
            state["copy"].start()

            def keep(j):
                index, total = value(j, bit_of(bit))
                acc[index] = total

            if k > 0:
                each(n, keep)

        return step

    near, rest = [0], list(range(1, bits))
    first = near + rest
    second = near + rest[1::-1] + rest[2:]
    third = near + rest[2:3] + rest[:2] + rest[3:]
    half = chans // 2
    post_1 = chain(0, first, out_post, slice(0, half))
    post_2 = chain(1, second, out_post, slice(half, chans))
    middle = chain(2, third, out_coarse, slice(0, chans))
    prior_1 = chain(3, first, out_prior, slice(0, chans))
    prior_2 = chain(4, second, out_prior, slice(chans, 2 * chans))
    parts_post = ((sums[0], 0), (sums[1], half))
    parts_coarse = ((sums[2], 0),)
    parts_prior = ((sums[3], 0), (sums[4], chans))

    def spread(parts, start, values):
        height = values.shape[0]
        for acc, at in parts:
            per, width = acc.shape[1:]
            row = start
            while row < start + height:
                inner = row % per
                size = min(per - inner, start + height - row)
                acc[row // per, inner : inner + size] = values[
                    row - start : row - start + size, at : at + width
                ]
                row += size

    def exchange(index, s, x, edges, slot, height, width, work_1=None, work_2=None):
        stride = width + 2 * EDGE
        depth = s.shape[0] * LANES

        def copy(src, dst, k, device):
            return pltpu.make_async_remote_copy(
                src_ref=src,
                dst_ref=dst,
                send_sem=sems.at[index, k],
                recv_sem=sems.at[index, 4 + k],
                device_id=device,
                device_id_type=pl.DeviceIdType.MESH,
            )

        edges[slot, 0] = get(s, pl.ds(EDGE, height, stride=stride)).astype(BF16)
        edges[slot, 1] = get(s, pl.ds(EDGE + width - 1, height, stride=stride)).astype(BF16)
        leftward = copy(edges.at[slot, 0], edges.at[slot, 3], 0, {"col": c - 1})
        rightward = copy(edges.at[slot, 1], edges.at[slot, 2], 1, {"col": c + 1})
        pl.when(has_left)(leftward.start)
        pl.when(has_right)(rightward.start)
        for i in range(height):
            x[pl.ds((i + 1) * width, width), depth : 2 * depth] = get(
                s, pl.ds(i * stride + EDGE, width)
            ).astype(BF16)
        if work_1 is not None:
            work_1()

        @pl.when(has_left)
        def _():
            leftward.wait_send()
            rightward.wait_recv()

        @pl.when(has_right)
        def _():
            rightward.wait_send()
            leftward.wait_recv()

        put(s, pl.ds(EDGE - 1, height, stride=stride), edges[slot, 2].astype(F32))
        put(s, pl.ds(EDGE + width, height, stride=stride), edges[slot, 3].astype(F32))
        order = [0, height - 1] + list(range(1, height - 1))
        upward = copy(
            x.at[pl.ds(width, width)], x.at[pl.ds((height + 1) * width, width)], 2, {"row": r - 1}
        )
        downward = copy(
            x.at[pl.ds(height * width, width)], x.at[pl.ds(0, width)], 3, {"row": r + 1}
        )
        for n, i in enumerate(order):
            for b in (0, 2):
                x[pl.ds((i + 1) * width, width), b * depth : (b + 1) * depth] = get(
                    s, pl.ds(i * stride + EDGE - 1 + b, width)
                ).astype(BF16)
            if n == 1:
                pl.when(has_up)(upward.start)
                pl.when(has_down)(downward.start)
        if work_2 is not None:
            work_2()

        @pl.when(has_up)
        def _():
            upward.wait_send()
            downward.wait_recv()

        @pl.when(has_down)
        def _():
            downward.wait_send()
            upward.wait_recv()

    def conv(x, w, start, size, width):
        k = w.shape[0] // 3
        total = None
        for a in range(3):
            part = jnp.dot(
                x[pl.ds(start + a * width, size), :],
                w[a * k : (a + 1) * k, :],
                preferred_element_type=F32,
            )
            total = part if total is None else total + part
        return total

    def conv_back(x, w, start, size, width):
        k = w.shape[0] // 9
        depth = w.shape[1]
        total = None
        for a in range(3):
            for b in range(3):
                tap = 3 * (2 - a) + (2 - b)
                part = lax.dot_general(
                    x[pl.ds(start + a * width, size), b * depth : (b + 1) * depth],
                    w[tap * k : (tap + 1) * k, :],
                    (((1,), (1,)), ((), ())),
                    preferred_element_type=F32,
                )
                total = part if total is None else total + part
        return total

    def weight_grad(x, g, parts, height, width, taps):
        depth = x.shape[1] // 3
        g_depth = g.shape[1] // 3
        size = height * width
        own = g[pl.ds(width, size), g_depth : 2 * g_depth]
        for a in taps:
            for b in range(3):
                tap = 3 * a + b
                values = scale * lax.dot_general(
                    x[pl.ds(a * width, size), b * depth : (b + 1) * depth],
                    own,
                    (((0,), (0,)), ((), ())),
                    preferred_element_type=F32,
                )
                spread(parts, tap * depth, values)

    lines = 8
    block = lines * cols
    half_block = block // 4

    def pool_sum(values):
        paired = values.reshape(lines // 2, 2, cols, chans)
        put(mix, pl.ds(0, block // 2), (paired[:, 0] + paired[:, 1]).reshape(block // 2, chans))
        return get(mix, pl.ds(0, half_block, stride=2)) + get(mix, pl.ds(1, half_block, stride=2))

    def repeat_columns(values):
        put(mix, pl.ds(0, half_rows * half_cols, stride=2), values)
        put(mix, pl.ds(1, half_rows * half_cols, stride=2), values)

    fine_stride = cols + 2 * EDGE
    half_stride = half_cols + 2 * EDGE

    for i in range(rows):
        put(s_feat, pl.ds(i * fine_stride + EDGE, cols), feat[pl.ds(i * cols, cols), :].astype(F32))
    exchange(0, s_feat, x_feat, edge_fine, 0, rows, cols)

    for m in range(rows // lines):
        values = conv(x_feat, w_post, m * block, block, cols) + noise_fine[pl.ds(m * block, block), :]
        fine[pl.ds(m * block, block), :] = values
        pooled = (0.25 * pool_sum(values)).astype(BF16).astype(F32)
        for i in range(lines // 2):
            at = pl.ds((m * lines // 2 + i) * half_stride + EDGE, half_cols)
            put(s_pool, at, pooled[i * half_cols : (i + 1) * half_cols])
    exchange(1, s_pool, x_pool, edge_coarse, 0, half_rows, half_cols)

    values = conv(x_pool, w_coarse, 0, half_rows * half_cols, half_cols) + noise_coarse[...]
    coarse[...] = values
    repeat_columns(values.astype(BF16).astype(F32))
    for i in range(rows):
        put(s_ctx, pl.ds(i * fine_stride + EDGE, cols), get(mix, pl.ds(i // 2 * cols, cols)))
    exchange(2, s_ctx, x_ctx, edge_fine, 1, rows, cols)

    for m in range(rows // lines):
        prior = conv(x_ctx, w_prior, m * block, block, cols)
        raw = prior[:, chans:]
        small = jnp.exp(-jnp.abs(raw))
        sigma = jnp.maximum(raw, 0.0) + jnp.log1p(small) + 0.5
        gate = jnp.where(raw >= 0, 1.0, small) / (1.0 + small)
        inverse = 1.0 / sigma
        deviation = fine[pl.ds(m * block, block), :] - prior[:, :chans]
        ratio = deviation * inverse
        residual = ratio * inverse
        err[pl.ds(m * block, block), :] = residual
        slope = (inverse - ratio * ratio * inverse) * gate
        for i in range(lines):
            at = pl.ds((m * lines + i) * fine_stride + EDGE, cols)
            here = slice(i * cols, (i + 1) * cols)
            both = jnp.concatenate([-residual[here], slope[here]], axis=1)
            put(s_dpr, at, both.astype(BF16).astype(F32))
    exchange(
        3,
        s_dpr,
        x_dpr,
        edge_dpr,
        0,
        rows,
        cols,
        lambda: weight_grad(x_ctx, x_dpr, parts_prior, rows, cols, (0, 1)),
        lambda: weight_grad(x_ctx, x_dpr, parts_prior, rows, cols, (2,)),
    )

    prior_1()
    prior_2()
    for m in range(rows // lines):
        if m == 3:
            prior_1()
            prior_2()
        back = pool_sum(conv_back(x_dpr, w_prior, m * block, block, cols))
        g = (coarse[pl.ds(m * half_block, half_block), :] + back).astype(BF16).astype(F32)
        for i in range(lines // 2):
            at = pl.ds((m * lines // 2 + i) * half_stride + EDGE, half_cols)
            put(s_gco, at, g[i * half_cols : (i + 1) * half_cols])
    exchange(
        4,
        s_gco,
        x_gco,
        edge_coarse,
        1,
        half_rows,
        half_cols,
        lambda: weight_grad(x_pool, x_gco, parts_coarse, half_rows, half_cols, (0, 1)),
        lambda: weight_grad(x_pool, x_gco, parts_coarse, half_rows, half_cols, (2,)),
    )

    middle()
    repeat_columns(0.25 * conv_back(x_gco, w_coarse, 0, half_rows * half_cols, half_cols))
    for i in range(rows):
        total = err[pl.ds(i * cols, cols), :] + get(mix, pl.ds(i // 2 * cols, cols))
        put(s_gfi, pl.ds(i * fine_stride + EDGE, cols), total.astype(BF16).astype(F32))
    prior_1()
    prior_2()
    middle()
    exchange(
        5,
        s_gfi,
        x_gfi,
        edge_fine,
        2,
        rows,
        cols,
        lambda: weight_grad(x_feat, x_gfi, parts_post, rows, cols, (0, 1)),
        lambda: weight_grad(x_feat, x_gfi, parts_post, rows, cols, (2,)),
    )
    post_1()
    post_2()
    prior_1()
    prior_2()
    for m in range(rows // lines):
        if m == 2:
            post_1()
            post_2()
            middle()
        grad_feat[pl.ds(m * block, block), :] = conv_back(
            x_gfi, w_post, m * block, block, cols
        ).astype(BF16)
    for _ in range(bits + 1):
        for step in (prior_1, prior_2, middle, post_1, post_2):
            step()


def on_device(sizes, feat, noise_fine, noise_coarse, w_post, w_coarse, w_prior):
    n_row, n_col = sizes
    rows, cols, chans = feat.shape
    half_rows, half_cols = rows // 2, cols // 2
    scale = 1.0 / math.sqrt(rows * n_row * cols * n_col)
    cells, half_cells = rows * cols, half_rows * half_cols
    vmem = pl.BlockSpec(memory_space=pltpu.VMEM)

    def padded(height, width, depth):
        return pltpu.VMEM((depth // LANES, height * (width + 2 * EDGE), LANES), F32)

    def columns(height, width, depth):
        return pltpu.VMEM(((height + 2) * width, 3 * depth), BF16)

    dims = (rows, cols, chans, scale, n_row, n_col)
    count = n_row * n_col
    per = w_post.shape[0] // count
    widths = (chans // 2, chans // 2, chans, chans, chans)
    grad_feat, out_post, out_coarse, out_prior = pl.pallas_call(
        functools.partial(tile_kernel, dims),
        out_shape=(
            jax.ShapeDtypeStruct((cells, chans), BF16),
            jax.ShapeDtypeStruct((per, chans), F32),
            jax.ShapeDtypeStruct((per, chans), F32),
            jax.ShapeDtypeStruct((per, 2 * chans), F32),
        ),
        in_specs=[vmem] * 6,
        out_specs=(vmem,) * 4,
        scratch_shapes=[
            pltpu.VMEM((cells, chans), F32),
            pltpu.VMEM((cells, chans), F32),
            pltpu.VMEM((half_cells, chans), F32),
            pltpu.VMEM((chans // LANES, 2 * half_cells, LANES), F32),
            padded(rows, cols, chans),
            padded(half_rows, half_cols, chans),
            padded(rows, cols, 2 * chans),
            columns(rows, cols, chans),
            columns(half_rows, half_cols, chans),
            columns(rows, cols, chans),
            columns(rows, cols, 2 * chans),
            columns(half_rows, half_cols, chans),
            columns(rows, cols, chans),
            pltpu.VMEM((3, 4, rows, chans), BF16),
            pltpu.VMEM((2, 4, half_rows, chans), BF16),
            pltpu.VMEM((1, 4, rows, 2 * chans), BF16),
            [pltpu.VMEM((count, per, width), F32) for width in widths],
            [pltpu.VMEM((count - 1, per, width), BF16) for width in widths],
            [pltpu.VMEM((count - 1, per, width), BF16) for width in widths],
            pltpu.SemaphoreType.DMA((6, 8)),
            pltpu.SemaphoreType.DMA((5, count.bit_length() - 1, 2)),
        ],
        compiler_params=pltpu.CompilerParams(
            collective_id=0, has_side_effects=True, vmem_limit_bytes=65000 * 1024
        ),
    )(
        feat.reshape(cells, chans),
        noise_fine.reshape(cells, chans),
        noise_coarse.reshape(half_cells, chans),
        w_post,
        w_coarse,
        w_prior,
    )
    return (
        grad_feat.reshape(rows, cols, chans),
        out_post.reshape(-1),
        out_coarse.reshape(-1),
        out_prior.reshape(-1),
    )


def solution(mesh):
    sizes = (mesh.shape["row"], mesh.shape["col"])
    return jax.shard_map(
        functools.partial(on_device, sizes),
        mesh=mesh,
        in_specs=(
            P("row", "col", None),
            P("row", "col", None),
            P("row", "col", None),
            P(),
            P(),
            P(),
        ),
        out_specs=(P("row", "col", None), P(("row", "col")), P(("row", "col")), P(("row", "col"))),
        check_vma=False,
    )
```

```python
import functools
import math

import jax
import jax.numpy as jnp
from jax import lax
from jax.experimental import pallas as pl
from jax.experimental.pallas import tpu as pltpu
from jax.sharding import PartitionSpec as P

F32 = jnp.float32
BF16 = jnp.bfloat16
EDGE = 8


LANES = 128


def put(ref, at, values):
    for d in range(ref.shape[0]):
        ref[d, at, :] = values[:, d * LANES : (d + 1) * LANES]


def get(ref, at):
    return jnp.concatenate([ref[d, at, :] for d in range(ref.shape[0])], axis=1)


def tile_kernel(
    dims,
    feat,
    noise_fine,
    noise_coarse,
    w_post,
    w_coarse,
    w_prior,
    grad_feat,
    out_post,
    out_coarse,
    out_prior,
    fine,
    err,
    coarse,
    mix,
    s_feat,
    s_pool,
    s_dpr,
    x_feat,
    x_pool,
    x_ctx,
    x_dpr,
    x_gco,
    x_gfi,
    edge_fine,
    edge_coarse,
    edge_dpr,
    sums,
    outgoing,
    incoming,
    sems,
    chain_sems,
):
    s_ctx = s_gfi = s_feat
    s_gco = s_pool
    rows, cols, chans, scale, n_row, n_col = dims
    half_rows, half_cols = rows // 2, cols // 2
    r = lax.axis_index("row")
    c = lax.axis_index("col")
    has_up, has_down = r > 0, r < n_row - 1
    has_left, has_right = c > 0, c < n_col - 1
    sides = (
        (has_up, {"row": r - 1}),
        (has_down, {"row": r + 1}),
        (has_left, {"col": c - 1}),
        (has_right, {"col": c + 1}),
    )
    edge_fine[...] = jnp.zeros_like(edge_fine)
    edge_coarse[...] = jnp.zeros_like(edge_coarse)
    edge_dpr[...] = jnp.zeros_like(edge_dpr)
    for x, width, height in (
        (x_feat, cols, rows),
        (x_pool, half_cols, half_rows),
        (x_ctx, cols, rows),
        (x_dpr, cols, rows),
        (x_gco, half_cols, half_rows),
        (x_gfi, cols, rows),
    ):
        x[0:width, :] = jnp.zeros((width, x.shape[1]), x.dtype)
        x[(height + 1) * width :, :] = jnp.zeros((width, x.shape[1]), x.dtype)

    barrier = pltpu.get_barrier_semaphore()
    for has, device in sides:
        @pl.when(has)
        def _(device=device):
            pl.semaphore_signal(
                barrier, inc=1, device_id=device, device_id_type=pl.DeviceIdType.MESH
            )
    count = n_row * n_col
    bits = count.bit_length() - 1
    col_bits = n_col.bit_length() - 1
    me = r * n_col + c

    def bit_of(b):
        return me // 2**b % 2

    def partner(b):
        if b < col_bits:
            return {"col": c + 2**b * (1 - 2 * bit_of(b))}
        return {"row": r + 2 ** (b - col_bits) * (1 - 2 * bit_of(b))}

    for b in range(bits):
        pl.semaphore_signal(
            barrier, inc=1, device_id=partner(b), device_id_type=pl.DeviceIdType.MESH
        )
    pl.semaphore_wait(barrier, bits + sum(has.astype(jnp.int32) for has, _device in sides))

    def each(n, body):
        if n <= 16:
            for j in range(n):
                body(j)
        else:
            pl.loop(0, n)(body)

    def chain(number, order, out, out_at):
        acc, send, recv = sums[number], outgoing[number], incoming[number]
        state = {"step": 0, "copy": None}

        def offset(k):
            return count - (count >> k)

        def step():
            k = state["step"]
            if k > bits:
                return
            state["step"] = k + 1
            if k > 0:
                state["copy"].wait()
            if k == bits:
                total = acc[me] + recv[offset(k - 1)].astype(F32)
                per = total.shape[0]
                stride = out.shape[0] // per
                for d in range(total.shape[1] // LANES):
                    out[pl.ds(out_at // LANES + d, per, stride=stride), :] = total[
                        :, d * LANES : (d + 1) * LANES
                    ]
                return
            bit = order[k]
            free = [b for b in range(bits) if b not in order[:k]]
            rest = [b for b in free if b != bit]
            place = free.index(bit)
            fixed = sum((bit_of(b) * 2**b for b in order[:k]), 0)
            n = count >> (k + 1)

            def value(j, choice):
                index = fixed + choice * 2**bit
                for q, b in enumerate(rest):
                    index = index + j // 2**q % 2 * 2**b
                total = acc[index]
                if k > 0:
                    slot = j // 2**place * 2 ** (place + 1) + choice * 2**place + j % 2**place
                    total = total + recv[offset(k - 1) + slot].astype(F32)
                return index, total

            def fill(j):
                send[offset(k) + j] = value(j, 1 - bit_of(bit))[1].astype(BF16)

            each(n, fill)
            state["copy"] = pltpu.make_async_remote_copy(
                src_ref=send.at[pl.ds(offset(k), n)],
                dst_ref=recv.at[pl.ds(offset(k), n)],
                send_sem=chain_sems.at[number, k, 0],
                recv_sem=chain_sems.at[number, k, 1],
                device_id=partner(bit),
                device_id_type=pl.DeviceIdType.MESH,
            )
            state["copy"].start()

            def keep(j):
                index, total = value(j, bit_of(bit))
                acc[index] = total

            if k > 0:
                each(n, keep)

        return step

    near, rest = [0], list(range(1, bits))
    first = near + rest
    second = near + rest[1::-1] + rest[2:]
    third = near + rest[2:3] + rest[:2] + rest[3:]
    half = chans // 2
    post_1 = chain(0, first, out_post, 0)
    post_2 = chain(1, second, out_post, half)
    middle = chain(2, third, out_coarse, 0)
    prior_1 = chain(3, first, out_prior, 0)
    prior_2 = chain(4, second, out_prior, chans)
    parts_post = ((sums[0], 0), (sums[1], half))
    parts_coarse = ((sums[2], 0),)
    parts_prior = ((sums[3], 0), (sums[4], chans))

    def spread(parts, start, values):
        height = values.shape[0]
        for acc, at in parts:
            per, width = acc.shape[1:]
            row = start
            while row < start + height:
                inner = row % per
                size = min(per - inner, start + height - row)
                acc[row // per, inner : inner + size] = values[
                    row - start : row - start + size, at : at + width
                ]
                row += size

    def exchange(index, s, x, edges, slot, height, width, work_1=None, work_2=None):
        stride = width + 2 * EDGE
        depth = s.shape[0] * LANES

        def copy(src, dst, k, device):
            return pltpu.make_async_remote_copy(
                src_ref=src,
                dst_ref=dst,
                send_sem=sems.at[index, k],
                recv_sem=sems.at[index, 4 + k],
                device_id=device,
                device_id_type=pl.DeviceIdType.MESH,
            )

        edges[slot, 0] = get(s, pl.ds(EDGE, height, stride=stride)).astype(BF16)
        edges[slot, 1] = get(s, pl.ds(EDGE + width - 1, height, stride=stride)).astype(BF16)
        leftward = copy(edges.at[slot, 0], edges.at[slot, 3], 0, {"col": c - 1})
        rightward = copy(edges.at[slot, 1], edges.at[slot, 2], 1, {"col": c + 1})
        pl.when(has_left)(leftward.start)
        pl.when(has_right)(rightward.start)
        for i in range(height):
            x[pl.ds((i + 1) * width, width), depth : 2 * depth] = get(
                s, pl.ds(i * stride + EDGE, width)
            ).astype(BF16)
        if work_1 is not None:
            work_1()

        @pl.when(has_left)
        def _():
            leftward.wait_send()
            rightward.wait_recv()

        @pl.when(has_right)
        def _():
            rightward.wait_send()
            leftward.wait_recv()

        put(s, pl.ds(EDGE - 1, height, stride=stride), edges[slot, 2].astype(F32))
        put(s, pl.ds(EDGE + width, height, stride=stride), edges[slot, 3].astype(F32))
        order = [0, height - 1] + list(range(1, height - 1))
        upward = copy(
            x.at[pl.ds(width, width)], x.at[pl.ds((height + 1) * width, width)], 2, {"row": r - 1}
        )
        downward = copy(
            x.at[pl.ds(height * width, width)], x.at[pl.ds(0, width)], 3, {"row": r + 1}
        )
        for n, i in enumerate(order):
            for b in (0, 2):
                x[pl.ds((i + 1) * width, width), b * depth : (b + 1) * depth] = get(
                    s, pl.ds(i * stride + EDGE - 1 + b, width)
                ).astype(BF16)
            if n == 1:
                pl.when(has_up)(upward.start)
                pl.when(has_down)(downward.start)
        if work_2 is not None:
            work_2()

        @pl.when(has_up)
        def _():
            upward.wait_send()
            downward.wait_recv()

        @pl.when(has_down)
        def _():
            downward.wait_send()
            upward.wait_recv()

    def conv(x, w, start, size, width):
        k = w.shape[0] // 3
        total = None
        for a in range(3):
            part = jnp.dot(
                x[pl.ds(start + a * width, size), :],
                w[a * k : (a + 1) * k, :],
                preferred_element_type=F32,
            )
            total = part if total is None else total + part
        return total

    def conv_back(x, w, start, size, width):
        k = w.shape[0] // 9
        depth = w.shape[1]
        total = None
        for a in range(3):
            for b in range(3):
                tap = 3 * (2 - a) + (2 - b)
                part = lax.dot_general(
                    x[pl.ds(start + a * width, size), b * depth : (b + 1) * depth],
                    w[tap * k : (tap + 1) * k, :],
                    (((1,), (1,)), ((), ())),
                    preferred_element_type=F32,
                )
                total = part if total is None else total + part
        return total

    def weight_grad(x, g, parts, height, width, taps):
        depth = x.shape[1] // 3
        g_depth = g.shape[1] // 3
        size = height * width
        own = g[pl.ds(width, size), g_depth : 2 * g_depth]
        for a in taps:
            for b in range(3):
                tap = 3 * a + b
                values = scale * lax.dot_general(
                    x[pl.ds(a * width, size), b * depth : (b + 1) * depth],
                    own,
                    (((0,), (0,)), ((), ())),
                    preferred_element_type=F32,
                )
                spread(parts, tap * depth, values)

    lines = 8
    block = lines * cols
    half_block = block // 4

    def pool_sum(values):
        paired = values.reshape(lines // 2, 2, cols, chans)
        put(mix, pl.ds(0, block // 2), (paired[:, 0] + paired[:, 1]).reshape(block // 2, chans))
        return get(mix, pl.ds(0, half_block, stride=2)) + get(mix, pl.ds(1, half_block, stride=2))

    def repeat_columns(values):
        put(mix, pl.ds(0, half_rows * half_cols, stride=2), values)
        put(mix, pl.ds(1, half_rows * half_cols, stride=2), values)

    fine_stride = cols + 2 * EDGE
    half_stride = half_cols + 2 * EDGE

    for i in range(rows):
        put(s_feat, pl.ds(i * fine_stride + EDGE, cols), feat[pl.ds(i * cols, cols), :].astype(F32))
    exchange(0, s_feat, x_feat, edge_fine, 0, rows, cols)

    for m in range(rows // lines):
        values = conv(x_feat, w_post, m * block, block, cols) + noise_fine[pl.ds(m * block, block), :]
        fine[pl.ds(m * block, block), :] = values
        pooled = (0.25 * pool_sum(values)).astype(BF16).astype(F32)
        for i in range(lines // 2):
            at = pl.ds((m * lines // 2 + i) * half_stride + EDGE, half_cols)
            put(s_pool, at, pooled[i * half_cols : (i + 1) * half_cols])
    exchange(1, s_pool, x_pool, edge_coarse, 0, half_rows, half_cols)

    values = conv(x_pool, w_coarse, 0, half_rows * half_cols, half_cols) + noise_coarse[...]
    coarse[...] = values
    repeat_columns(values.astype(BF16).astype(F32))
    for i in range(rows):
        put(s_ctx, pl.ds(i * fine_stride + EDGE, cols), get(mix, pl.ds(i // 2 * cols, cols)))
    exchange(2, s_ctx, x_ctx, edge_fine, 1, rows, cols)

    for m in range(rows // lines):
        prior = conv(x_ctx, w_prior, m * block, block, cols)
        raw = prior[:, chans:]
        small = jnp.exp(-jnp.abs(raw))
        sigma = jnp.maximum(raw, 0.0) + jnp.log1p(small) + 0.5
        gate = jnp.where(raw >= 0, 1.0, small) / (1.0 + small)
        inverse = 1.0 / sigma
        deviation = fine[pl.ds(m * block, block), :] - prior[:, :chans]
        ratio = deviation * inverse
        residual = ratio * inverse
        err[pl.ds(m * block, block), :] = residual
        slope = (inverse - ratio * ratio * inverse) * gate
        for i in range(lines):
            at = pl.ds((m * lines + i) * fine_stride + EDGE, cols)
            here = slice(i * cols, (i + 1) * cols)
            both = jnp.concatenate([-residual[here], slope[here]], axis=1)
            put(s_dpr, at, both.astype(BF16).astype(F32))
    exchange(
        3,
        s_dpr,
        x_dpr,
        edge_dpr,
        0,
        rows,
        cols,
        lambda: weight_grad(x_ctx, x_dpr, parts_prior, rows, cols, (0, 1)),
        lambda: weight_grad(x_ctx, x_dpr, parts_prior, rows, cols, (2,)),
    )

    prior_1()
    prior_2()
    for m in range(rows // lines):
        if m == 2:
            prior_1()
            prior_2()
        back = pool_sum(conv_back(x_dpr, w_prior, m * block, block, cols))
        g = (coarse[pl.ds(m * half_block, half_block), :] + back).astype(BF16).astype(F32)
        for i in range(lines // 2):
            at = pl.ds((m * lines // 2 + i) * half_stride + EDGE, half_cols)
            put(s_gco, at, g[i * half_cols : (i + 1) * half_cols])
    exchange(
        4,
        s_gco,
        x_gco,
        edge_coarse,
        1,
        half_rows,
        half_cols,
        lambda: weight_grad(x_pool, x_gco, parts_coarse, half_rows, half_cols, (0, 1)),
        lambda: weight_grad(x_pool, x_gco, parts_coarse, half_rows, half_cols, (2,)),
    )

    prior_1()
    prior_2()
    middle()
    repeat_columns(0.25 * conv_back(x_gco, w_coarse, 0, half_rows * half_cols, half_cols))
    for i in range(rows):
        total = err[pl.ds(i * cols, cols), :] + get(mix, pl.ds(i // 2 * cols, cols))
        put(s_gfi, pl.ds(i * fine_stride + EDGE, cols), total.astype(BF16).astype(F32))
    def late_work():
        prior_1()
        prior_2()
        middle()
        weight_grad(x_feat, x_gfi, parts_post, rows, cols, (2,))

    exchange(
        5,
        s_gfi,
        x_gfi,
        edge_fine,
        2,
        rows,
        cols,
        lambda: weight_grad(x_feat, x_gfi, parts_post, rows, cols, (0, 1)),
        late_work,
    )
    post_1()
    post_2()
    for m in range(rows // lines):
        if m == 2:
            post_1()
            post_2()
            prior_1()
            prior_2()
        grad_feat[pl.ds(m * block, block), :] = conv_back(
            x_gfi, w_post, m * block, block, cols
        ).astype(BF16)
    for _ in range(bits + 1):
        for step in (prior_1, prior_2, middle, post_1, post_2):
            step()


def hand_out(*refs):
    for source, target in zip(refs[:4], refs[4:]):
        target[...] = source[...]


def on_device(sizes, feat, noise_fine, noise_coarse, w_post, w_coarse, w_prior):
    n_row, n_col = sizes
    rows, cols, chans = feat.shape
    half_rows, half_cols = rows // 2, cols // 2
    scale = 1.0 / math.sqrt(rows * n_row * cols * n_col)
    cells, half_cells = rows * cols, half_rows * half_cols
    vmem = pl.BlockSpec(memory_space=pltpu.VMEM)

    def padded(height, width, depth):
        return pltpu.VMEM((depth // LANES, height * (width + 2 * EDGE), LANES), F32)

    def columns(height, width, depth):
        return pltpu.VMEM(((height + 2) * width, 3 * depth), BF16)

    dims = (rows, cols, chans, scale, n_row, n_col)
    count = n_row * n_col
    per = w_post.shape[0] // count
    widths = (chans // 2, chans // 2, chans, chans, chans)
    grad_feat, out_post, out_coarse, out_prior = pl.pallas_call(
        functools.partial(tile_kernel, dims),
        out_shape=(
            jax.ShapeDtypeStruct((cells, chans), BF16),
            jax.ShapeDtypeStruct((per * chans // LANES, LANES), F32),
            jax.ShapeDtypeStruct((per * chans // LANES, LANES), F32),
            jax.ShapeDtypeStruct((per * 2 * chans // LANES, LANES), F32),
        ),
        in_specs=[vmem] * 6,
        out_specs=(vmem,) * 4,
        scratch_shapes=[
            pltpu.VMEM((cells, chans), F32),
            pltpu.VMEM((cells, chans), F32),
            pltpu.VMEM((half_cells, chans), F32),
            pltpu.VMEM((chans // LANES, 2 * half_cells, LANES), F32),
            padded(rows, cols, chans),
            padded(half_rows, half_cols, chans),
            padded(rows, cols, 2 * chans),
            columns(rows, cols, chans),
            columns(half_rows, half_cols, chans),
            columns(rows, cols, chans),
            columns(rows, cols, 2 * chans),
            columns(half_rows, half_cols, chans),
            columns(rows, cols, chans),
            pltpu.VMEM((3, 4, rows, chans), BF16),
            pltpu.VMEM((2, 4, half_rows, chans), BF16),
            pltpu.VMEM((1, 4, rows, 2 * chans), BF16),
            [pltpu.VMEM((count, per, width), F32) for width in widths],
            [pltpu.VMEM((count - 1, per, width), BF16) for width in widths],
            [pltpu.VMEM((count - 1, per, width), BF16) for width in widths],
            pltpu.SemaphoreType.DMA((6, 8)),
            pltpu.SemaphoreType.DMA((5, count.bit_length() - 1, 2)),
        ],
        compiler_params=pltpu.CompilerParams(
            collective_id=0, has_side_effects=True, vmem_limit_bytes=65000 * 1024
        ),
    )(
        feat.reshape(cells, chans),
        noise_fine.reshape(cells, chans),
        noise_coarse.reshape(half_cells, chans),
        w_post,
        w_coarse,
        w_prior,
    )
    results = (grad_feat, out_post, out_coarse, out_prior)
    grad_feat, out_post, out_coarse, out_prior = pl.pallas_call(
        hand_out,
        out_shape=tuple(jax.ShapeDtypeStruct(a.shape, a.dtype) for a in results),
        in_specs=[vmem] * 4,
        out_specs=(vmem,) * 4,
    )(*results)
    return (
        grad_feat.reshape(rows, cols, chans),
        out_post.reshape(-1),
        out_coarse.reshape(-1),
        out_prior.reshape(-1),
    )


def solution(mesh):
    sizes = (mesh.shape["row"], mesh.shape["col"])
    return jax.shard_map(
        functools.partial(on_device, sizes),
        mesh=mesh,
        in_specs=(
            P("row", "col", None),
            P("row", "col", None),
            P("row", "col", None),
            P(),
            P(),
            P(),
        ),
        out_specs=(P("row", "col", None), P(("row", "col")), P(("row", "col")), P(("row", "col"))),
        check_vma=False,
    )
```
